32 devices in a mesh: row: 8 (over y, x, core), col: 4 (over z).
Axes of the slice: x: 2, y: 2, z: 4, core: 2. Of those that a mesh axis runs over, the one named last changes fastest.
Arguments:
- eigvec: float32 [8192, 1024], P('row', 'col'), may hold values from -6 to 6
- refl: float32 [4, 8192, 256], P(None, ('row', 'col')), may hold values from -0.25 to 0.25
- tfac: float32 [4, 4096, 256], P(None, ('row', 'col')), may hold values from -0.375 to 0.375
- sched: int32 [16, 4], P('row'), may hold values from 0 to 3, each once within a row
Outputs:
- result: float32 [8192, 1024], P('row', 'col')
The draws below stay inside these ranges and needn't reach their ends.
Inputs may be any that keep to these rules, and one draw needn't show every extreme that they name: Each row of sched names every slot 0 to 3 exactly once.
All inputs are finite; a program needn't handle non-finite values.
Results may differ from the reference program's by a relative error of at most 0.0002.
Values sent between devices are 32-bit elements; how exact they have to be, the bound alone decides.
A program may use at most 64 MiB of HBM per device.

```python
import jax
import jax.numpy as jnp
from jax import lax

B = 512
W = 256
STEPS = 4
GROUPS = 16
ORDER = 8192
EVECS = 1024


def levels(stream_key, shape, cuts, least, top_value):
    def one(dim, parts):
        heights = jax.random.uniform(jax.random.fold_in(jax.random.fold_in(stream_key, 6), dim), (parts,), jnp.float32, least / len(cuts), top_value / len(cuts))
        return jnp.repeat(jnp.exp(heights), shape[dim] // parts).reshape((-1,) + (1,) * (len(shape) - dim - 1))

    gain = one(*cuts[0])
    for cut in cuts[1:]:
        gain = gain * one(*cut)
    return gain


def centred(stream_key, shape, width, limit, shards=(), kind=jnp.bfloat16):
    entries = jax.random.normal(stream_key, shape, jnp.float32) * width
    if len(shards) > 0:
        entries = levels(stream_key, shape, shards, -0.22, 0.18) * entries
    return jnp.clip(entries, min=-limit, max=limit).astype(kind)


def setup_inputs(seed: int = 0) -> dict:
    key_of = jax.random.split(jax.random.key(seed), 5)
    return {
        "eigvec": centred(key_of[0], (ORDER, EVECS), 1.0, 6.0, ((0, 8), (1, 4)), jnp.float32),
        "refl": centred(key_of[1], (STEPS, ORDER, W), B ** -0.5, 0.25, ((1, 32),), jnp.float32),
        "tfac": centred(key_of[2], (STEPS, GROUPS * W, W), W ** -0.5, 0.375, ((1, 32),), jnp.float32),
        "sched": jax.vmap(lambda own: jax.random.permutation(own, STEPS))(jax.random.split(key_of[3], GROUPS)).reshape((GROUPS, STEPS)).astype(jnp.int32),
    }


def apply_blocks(field, vectors, factor):
    coupling = jnp.einsum('gbw,gbe->gwe', vectors, field, precision=lax.Precision.HIGHEST)
    coeffs = jnp.einsum('gvw,gwe->gve', factor, coupling, precision=lax.Precision.HIGHEST)
    return field - jnp.einsum('gbw,gwe->gbe', vectors, coeffs, precision=lax.Precision.HIGHEST)


def reference(eigvec, refl, tfac, sched):
    groups = sched.shape[0]
    evcount = eigvec.shape[1]
    stacked_v = refl.reshape(STEPS, groups, B, W)
    stacked_t = tfac.reshape(STEPS, groups, W, W)
    group_ids = jnp.arange(groups).astype(jnp.int32)
    field = eigvec
    for step_no in range(STEPS):
        slots = sched[:, step_no].astype(jnp.int32)
        vectors = stacked_v[slots, group_ids]
        factor = stacked_t[slots, group_ids]
        if step_no % 2 == 0:
            field = apply_blocks(field.reshape(groups, B, evcount), vectors, factor).reshape(groups * B, evcount)
        else:
            middle = field[W:groups * B - W].reshape(groups - 1, B, evcount)
            middle = apply_blocks(middle, vectors[:-1], factor[:-1]).reshape((groups - 1) * B, evcount)
            field = jnp.concatenate([field[:W], middle, field[groups * B - W:]], axis=0)
    return field
```

```python
import functools

import jax
import jax.numpy as jnp
from jax import lax
from jax.experimental import pallas as pl
from jax.experimental.pallas import tpu as pltpu
from jax.sharding import PartitionSpec as P

B = 512
W = 256
MESH = pl.DeviceIdType.MESH


def split(x):
    high = x.astype(jnp.bfloat16)
    low = (x - high.astype(jnp.float32)).astype(jnp.bfloat16)
    return high, low


def product(left, right, dims):
    def one(a, b):
        return lax.dot_general(a, b, (dims, ((), ())), preferred_element_type=jnp.float32)

    return one(left[0], right[0]) + (one(left[0], right[1]) + one(left[1], right[0]))


def pick_kernel(slots, refl, tfac, packed, hold, in_sem, out_sem):
    steps = packed.shape[0]
    v_rows = refl.shape[1]
    t_rows = tfac.shape[1]
    loads, stores = [], []
    for s in range(steps):
        slot = slots[s]
        loads.append(
            (
                pltpu.make_async_copy(refl.at[slot], hold.at[s, pl.ds(0, v_rows)], in_sem.at[s, 0]),
                pltpu.make_async_copy(tfac.at[slot], hold.at[s, pl.ds(v_rows, t_rows)], in_sem.at[s, 1]),
            )
        )
        stores.append(pltpu.make_async_copy(hold.at[s], packed.at[s], out_sem.at[s]))
    for pair in loads:
        for copy in pair:
            copy.start()
    for pair, store in zip(loads, stores):
        for copy in pair:
            copy.wait()
        store.start()
    for store in stores:
        store.wait()


def main_kernel(n, rows_n, groups, packed, eig, out, field, buf, inb, back, landed, own_sem, eig_sem, out_sem,
                ring_send, ring_recv, up_send, up_recv, down_send, down_recv):
    steps, piece, _ = packed.shape
    v_rows = groups * B // n
    per_group = n // groups
    half = piece // 2
    hops = n // 2
    row = lax.axis_index("row")
    col = lax.axis_index("col")
    right = lax.rem(col + 1, n)
    left = lax.rem(col + n - 1, n)
    has_down = row < rows_n - 1
    has_up = row > 0
    down = jnp.minimum(row + 1, rows_n - 1)
    up = jnp.maximum(row - 1, 0)

    eig_copy = pltpu.make_async_copy(eig, field, eig_sem)
    eig_copy.start()

    barrier = pltpu.get_barrier_semaphore()
    pl.semaphore_signal(barrier, inc=1, device_id=(row, left), device_id_type=MESH)
    pl.semaphore_signal(barrier, inc=1, device_id=(row, right), device_id_type=MESH)

    @pl.when(has_up)
    def _():
        pl.semaphore_signal(barrier, inc=1, device_id=(up, col), device_id_type=MESH)

    @pl.when(has_down)
    def _():
        pl.semaphore_signal(barrier, inc=1, device_id=(down, col), device_id_type=MESH)

    pl.semaphore_wait(barrier, 2 + jnp.minimum(row, 1) + jnp.minimum(rows_n - 1 - row, 1))

    def ring_copy(s, way, hop, part):
        target = right if way == 0 else left
        owner = lax.rem(col + n - hop, n) if way == 0 else lax.rem(col + hop, n)
        span = pl.ds(part * half, half)
        src = packed.at[s, span] if hop == 0 else buf.at[s, owner, span]
        return pltpu.make_async_remote_copy(
            src_ref=src,
            dst_ref=buf.at[s, owner, span],
            send_sem=ring_send.at[s, way, hop, part],
            recv_sem=ring_recv.at[s, way, hop, part],
            device_id=(row, target),
            device_id_type=MESH,
        )

    def parts_of(way, hop):
        order = (0, 1) if way == 0 else (1, 0)
        return order[:1] if hop == hops - 1 else order

    def send_own(s):
        for k in range(len(parts_of(0, 0))):
            for way in (0, 1):
                ring_copy(s, way, 0, parts_of(way, 0)[k]).start()

    def forward(s):
        for hop in range(1, hops):
            for k in range(len(parts_of(0, hop))):
                for way in (0, 1):
                    part = parts_of(way, hop)[k]
                    ring_copy(s, way, hop - 1, part).wait_recv()
                    ring_copy(s, way, hop, part).start()

    def finish(s):
        for hop in range(hops):
            for way in (0, 1):
                done = parts_of(way, hop + 1) if hop + 1 < hops else ()
                for part in parts_of(way, hop):
                    if part not in done:
                        ring_copy(s, way, hop, part).wait_recv()

    def vectors_of(s, g):
        block = buf[s, g * per_group:(g + 1) * per_group, :v_rows]
        return split(block.reshape(B, W))

    def factor_of(s, g):
        block = buf[s, g * per_group:(g + 1) * per_group, v_rows:]
        return split(block.reshape(W, W))

    def coeffs_of(s, g, vectors, rows):
        coupling = product(vectors, split(rows), ((0,), (0,)))
        return split(product(factor_of(s, g), split(coupling), ((1,), (0,))))

    def apply_local(s, g, start):
        vectors = vectors_of(s, g)
        rows = field[start:start + B]
        coeffs = coeffs_of(s, g, vectors, rows)
        field[start:start + B] = rows - product(vectors, coeffs, ((1,), (0,)))

    def up_copy(i):
        return pltpu.make_async_remote_copy(
            src_ref=field.at[pl.ds(0, W)], dst_ref=inb.at[i],
            send_sem=up_send.at[i], recv_sem=up_recv.at[i],
            device_id=(up, col), device_id_type=MESH,
        )

    def down_copy(i):
        return pltpu.make_async_remote_copy(
            src_ref=back.at[i], dst_ref=landed.at[i],
            send_sem=down_send.at[i], recv_sem=down_recv.at[i],
            device_id=(down, col), device_id_type=MESH,
        )

    low = groups * B - W

    send_own(0)
    own = [pltpu.make_async_copy(packed.at[s], buf.at[s, col], own_sem.at[s]) for s in range(steps)]
    for copy in own:
        copy.start()
    eig_copy.wait()
    for s in range(steps):
        forward(s)
        if s + 1 < steps:
            send_own(s + 1)
        own[s].wait()
        finish(s)
        i = s // 2
        if s % 2 == 0:
            for g in range(groups):
                apply_local(s, g, g * B)
                if g == 0 and s + 1 < steps:
                    @pl.when(has_up)
                    def _():
                        up_copy(i).start()
        else:
            @pl.when(has_down)
            def _():
                up_copy(i).wait_recv()
                g = groups - 1
                vectors = vectors_of(s, g)
                rows = jnp.concatenate([field[low:], inb[i]], axis=0)
                coeffs = coeffs_of(s, g, vectors, rows)
                bottom = (vectors[0][W:], vectors[1][W:])
                back[i] = rows[W:] - product(bottom, coeffs, ((1,), (0,)))
                down_copy(i).start()
                top = (vectors[0][:W], vectors[1][:W])
                field[low:] = rows[:W] - product(top, coeffs, ((1,), (0,)))

            for g in range(groups - 1):
                apply_local(s, g, W + g * B)

            @pl.when(has_up)
            def _():
                up_copy(i).wait_send()
                down_copy(i).wait_recv()
                field[:W] = landed[i]

    store = pltpu.make_async_copy(field, out, out_sem)
    store.start()
    for s in range(steps):
        for way in (0, 1):
            for hop in range(hops):
                for part in parts_of(way, hop):
                    ring_copy(s, way, hop, part).wait_send()

    @pl.when(has_down)
    def _():
        for i in range(steps // 2):
            down_copy(i).wait_send()

    store.wait()


def on_device(n, rows_n, eigvec, refl, tfac, sched):
    steps, v_rows, _ = refl.shape
    t_rows = tfac.shape[1]
    groups = sched.shape[0]
    evcount = eigvec.shape[1]
    piece = v_rows + t_rows
    hops = n // 2
    owner = lax.axis_index("col") * v_rows // B
    slots = lax.dynamic_index_in_dim(sched, owner, 0, keepdims=False)
    anywhere = pl.BlockSpec(memory_space=pl.ANY)
    packed = pl.pallas_call(
        pick_kernel,
        out_shape=jax.ShapeDtypeStruct((steps, piece, W), jnp.float32),
        in_specs=[pl.BlockSpec(memory_space=pltpu.SMEM), anywhere, anywhere],
        out_specs=anywhere,
        scratch_shapes=[
            pltpu.VMEM((steps, piece, W), jnp.float32),
            pltpu.SemaphoreType.DMA((steps, 2)),
            pltpu.SemaphoreType.DMA((steps,)),
        ],
        name="pick",
    )(slots, refl, tfac)
    half_steps = steps // 2
    return pl.pallas_call(
        functools.partial(main_kernel, n, rows_n, groups),
        out_shape=jax.ShapeDtypeStruct(eigvec.shape, jnp.float32),
        in_specs=[anywhere, anywhere],
        out_specs=anywhere,
        scratch_shapes=[
            pltpu.VMEM(eigvec.shape, jnp.float32),
            pltpu.VMEM((steps, n, piece, W), jnp.float32),
            pltpu.VMEM((half_steps, W, evcount), jnp.float32),
            pltpu.VMEM((half_steps, W, evcount), jnp.float32),
            pltpu.VMEM((half_steps, W, evcount), jnp.float32),
            pltpu.SemaphoreType.DMA((steps,)),
            pltpu.SemaphoreType.DMA,
            pltpu.SemaphoreType.DMA,
            pltpu.SemaphoreType.DMA((steps, 2, hops, 2)),
            pltpu.SemaphoreType.DMA((steps, 2, hops, 2)),
            pltpu.SemaphoreType.DMA((half_steps,)),
            pltpu.SemaphoreType.DMA((half_steps,)),
            pltpu.SemaphoreType.DMA((half_steps,)),
            pltpu.SemaphoreType.DMA((half_steps,)),
        ],
        compiler_params=pltpu.CompilerParams(
            collective_id=0, has_side_effects=True, vmem_limit_bytes=48 << 20
        ),
        name="sweep",
    )(packed, eigvec)


def solution(mesh):
    placed = (
        P("row", "col"),
        P(None, ("row", "col"), None),
        P(None, ("row", "col"), None),
        P("row", None),
    )
    body = functools.partial(on_device, mesh.shape["col"], mesh.shape["row"])
    return jax.shard_map(body, mesh=mesh, in_specs=placed, out_specs=P("row", "col"), check_vma=False)
```

```python
import functools

import jax
import jax.numpy as jnp
from jax import lax
from jax.experimental import pallas as pl
from jax.experimental.pallas import tpu as pltpu
from jax.sharding import PartitionSpec as P

B = 512
W = 256
MESH = pl.DeviceIdType.MESH


def split(x):
    high = x.astype(jnp.bfloat16)
    low = (x - high.astype(jnp.float32)).astype(jnp.bfloat16)
    return high, low


def product(left, right, dims):
    def one(a, b):
        return lax.dot_general(a, b, (dims, ((), ())), preferred_element_type=jnp.float32)

    return one(left[0], right[0]) + (one(left[0], right[1]) + one(left[1], right[0]))


def pick_kernel(slots, refl, tfac, packed, hold, in_sem, out_sem):
    steps = packed.shape[0]
    v_rows = refl.shape[1]
    t_rows = tfac.shape[1]
    loads, stores = [], []
    for s in range(steps):
        slot = slots[s]
        loads.append(
            (
                pltpu.make_async_copy(refl.at[slot], hold.at[s, pl.ds(0, v_rows)], in_sem.at[s, 0]),
                pltpu.make_async_copy(tfac.at[slot], hold.at[s, pl.ds(v_rows, t_rows)], in_sem.at[s, 1]),
            )
        )
        stores.append(pltpu.make_async_copy(hold.at[s], packed.at[s], out_sem.at[s]))
    for pair in loads:
        for copy in pair:
            copy.start()
    for pair, store in zip(loads, stores):
        for copy in pair:
            copy.wait()
        store.start()
    for store in stores:
        store.wait()


def main_kernel(n, rows_n, groups, packed, eig, out, field, buf, inb, back, landed, own_sem, eig_sem, out_sem,
                ring_send, ring_recv, up_send, up_recv, down_send, down_recv):
    steps, piece, _ = packed.shape
    v_rows = groups * B // n
    per_group = n // groups
    half = piece // 2
    hops = n // 2
    row = lax.axis_index("row")
    col = lax.axis_index("col")
    right = lax.rem(col + 1, n)
    left = lax.rem(col + n - 1, n)
    has_down = row < rows_n - 1
    has_up = row > 0
    down = jnp.minimum(row + 1, rows_n - 1)
    up = jnp.maximum(row - 1, 0)

    eig_copy = pltpu.make_async_copy(eig, field, eig_sem)
    eig_copy.start()

    barrier = pltpu.get_barrier_semaphore()
    pl.semaphore_signal(barrier, inc=1, device_id=(row, left), device_id_type=MESH)
    pl.semaphore_signal(barrier, inc=1, device_id=(row, right), device_id_type=MESH)

    @pl.when(has_up)
    def _():
        pl.semaphore_signal(barrier, inc=1, device_id=(up, col), device_id_type=MESH)

    @pl.when(has_down)
    def _():
        pl.semaphore_signal(barrier, inc=1, device_id=(down, col), device_id_type=MESH)

    pl.semaphore_wait(barrier, 2 + jnp.minimum(row, 1) + jnp.minimum(rows_n - 1 - row, 1))

    def ring_copy(s, way, hop, part):
        target = right if way == 0 else left
        owner = lax.rem(col + n - hop, n) if way == 0 else lax.rem(col + hop, n)
        span = pl.ds(part * half, half)
        src = packed.at[s, span] if hop == 0 else buf.at[s, owner, span]
        return pltpu.make_async_remote_copy(
            src_ref=src,
            dst_ref=buf.at[s, owner, span],
            send_sem=ring_send.at[s, way, hop, part],
            recv_sem=ring_recv.at[s, way, hop, part],
            device_id=(row, target),
            device_id_type=MESH,
        )

    def parts_of(way, hop):
        order = (0, 1) if way == 0 else (1, 0)
        return order[:1] if hop == hops - 1 else order

    def send_own(s):
        for k in range(len(parts_of(0, 0))):
            for way in (0, 1):
                ring_copy(s, way, 0, parts_of(way, 0)[k]).start()

    def forward(s):
        for hop in range(1, hops):
            for k in range(len(parts_of(0, hop))):
                for way in (0, 1):
                    part = parts_of(way, hop)[k]
                    ring_copy(s, way, hop - 1, part).wait_recv()
                    ring_copy(s, way, hop, part).start()

    def finish(s):
        for hop in range(hops):
            for way in (0, 1):
                done = parts_of(way, hop + 1) if hop + 1 < hops else ()
                for part in parts_of(way, hop):
                    if part not in done:
                        ring_copy(s, way, hop, part).wait_recv()

    def vectors_of(s, g):
        block = buf[s, g * per_group:(g + 1) * per_group, :v_rows]
        return split(block.reshape(B, W))

    def factor_of(s, g):
        block = buf[s, g * per_group:(g + 1) * per_group, v_rows:]
        return split(block.reshape(W, W))

    def coeffs_of(s, g, vectors, rows):
        coupling = product(vectors, split(rows), ((0,), (0,)))
        return split(product(factor_of(s, g), split(coupling), ((1,), (0,))))

    def apply_local(s, g, start):
        vectors = vectors_of(s, g)
        rows = field[start:start + B]
        coeffs = coeffs_of(s, g, vectors, rows)
        field[start:start + B] = rows - product(vectors, coeffs, ((1,), (0,)))

    def up_copy(i):
        return pltpu.make_async_remote_copy(
            src_ref=field.at[pl.ds(0, W)], dst_ref=inb.at[i],
            send_sem=up_send.at[i], recv_sem=up_recv.at[i],
            device_id=(up, col), device_id_type=MESH,
        )

    def down_copy(i):
        return pltpu.make_async_remote_copy(
            src_ref=back.at[i], dst_ref=landed.at[i],
            send_sem=down_send.at[i], recv_sem=down_recv.at[i],
            device_id=(down, col), device_id_type=MESH,
        )

    low = groups * B - W

    send_own(0)
    own = [pltpu.make_async_copy(packed.at[s], buf.at[s, col], own_sem.at[s]) for s in range(steps)]
    for copy in own:
        copy.start()
    eig_copy.wait()
    for s in range(steps):
        forward(s)
        if s + 1 < steps:
            send_own(s + 1)
        own[s].wait()
        finish(s)
        i = s // 2
        if s % 2 == 0:
            for g in range(groups):
                apply_local(s, g, g * B)
                if g == 0 and s + 1 < steps:
                    @pl.when(has_up)
                    def _():
                        up_copy(i).start()
        else:
            @pl.when(has_down)
            def _():
                up_copy(i).wait_recv()
                g = groups - 1
                vectors = vectors_of(s, g)
                rows = jnp.concatenate([field[low:], inb[i]], axis=0)
                coeffs = coeffs_of(s, g, vectors, rows)
                bottom = (vectors[0][W:], vectors[1][W:])
                back[i] = rows[W:] - product(bottom, coeffs, ((1,), (0,)))
                down_copy(i).start()
                top = (vectors[0][:W], vectors[1][:W])
                field[low:] = rows[:W] - product(top, coeffs, ((1,), (0,)))

            for g in range(groups - 1):
                apply_local(s, g, W + g * B)

            @pl.when(has_up)
            def _():
                up_copy(i).wait_send()
                down_copy(i).wait_recv()
                field[:W] = landed[i]

    store = pltpu.make_async_copy(field, out, out_sem)
    store.start()
    for s in range(steps):
        for way in (0, 1):
            for hop in range(hops):
                for part in parts_of(way, hop):
                    ring_copy(s, way, hop, part).wait_send()

    @pl.when(has_down)
    def _():
        for i in range(steps // 2):
            down_copy(i).wait_send()

    store.wait()


def line_kernel(rows_n, packed, eig, out, field, buf, inb, back, landed, own_sem, eig_sem, out_sem,
                feed_send, feed_recv, cols_send, cols_recv, cross_send, cross_recv,
                up_send, up_recv, down_send, down_recv, res_send, res_recv):
    steps, piece, _ = packed.shape
    v_rows = B // 2
    low = B + W
    last = steps - 1
    row = lax.axis_index("row")
    col = lax.axis_index("col")
    inner = (col == 1) | (col == 2)
    partner = col + 1 - 2 * lax.rem(col, 2)
    other = 3 - col
    has_down = row < rows_n - 1
    has_up = row > 0
    down = jnp.minimum(row + 1, rows_n - 1)
    up = jnp.maximum(row - 1, 0)

    def remote(src, dst, send, recv, target):
        return pltpu.make_async_remote_copy(
            src_ref=src, dst_ref=dst, send_sem=send, recv_sem=recv,
            device_id=target, device_id_type=MESH,
        )

    def greet(target):
        pl.semaphore_signal(barrier, inc=1, device_id=target, device_id_type=MESH)

    barrier = pltpu.get_barrier_semaphore()
    some_up = jnp.minimum(row, 1)
    some_down = jnp.minimum(rows_n - 1 - row, 1)
    greet((row, partner))

    @pl.when(inner)
    def _():
        greet((row, other))

        @pl.when(has_up)
        def _():
            greet((up, col))

        @pl.when(has_down)
        def _():
            greet((down, col))
            greet((down, partner))

    @pl.when(jnp.logical_not(inner) & has_up)
    def _():
        greet((up, partner))

    @pl.when(inner)
    def _():
        pl.semaphore_wait(barrier, 2 + some_up + 2 * some_down)

    @pl.when(jnp.logical_not(inner))
    def _():
        pl.semaphore_wait(barrier, 1 + some_up)

    def feed(s, owner):
        return remote(packed.at[s], buf.at[s, owner], feed_send.at[s], feed_recv.at[s], (row, partner))

    columns = remote(eig, field.at[1], cols_send, cols_recv, (row, partner))

    def cross(s, k):
        owner = col if k == 0 else partner
        src = packed.at[s] if k == 0 else buf.at[s, owner]
        return remote(src, buf.at[s, owner], cross_send.at[s, k], cross_recv.at[s, k], (row, other))

    def result(part, src, target_row):
        span = (pl.ds(0, W), pl.ds(W, B), pl.ds(low, W))[part]
        return remote(src, out.at[span], res_send.at[part], res_recv.at[part], (target_row, partner))

    @pl.when(jnp.logical_not(inner))
    def _():
        feed(0, col).start()
        feed(1, col).start()
        columns.start()
        for s in range(2, steps):
            feed(s, col).start()
        for s in range(steps):
            feed(s, col).wait_send()
        columns.wait_send()
        for part in range(3):
            rows = (W, B, W)[part]
            result(part, field.at[0, pl.ds(0, rows)], row).wait_recv()

    def vectors_of(s, g):
        return split(buf[s, 2 * g:2 * g + 2, :v_rows].reshape(B, W))

    def factor_of(s, g):
        return split(buf[s, 2 * g:2 * g + 2, v_rows:].reshape(W, W))

    def coeffs_of(vectors, factor, rows):
        coupling = product(vectors, split(rows), ((0,), (0,)))
        return split(product(factor, split(coupling), ((1,), (0,))))

    def apply_local(s, g, z, start):
        vectors = vectors_of(s, g)
        rows = field[z, start:start + B]
        coeffs = coeffs_of(vectors, factor_of(s, g), rows)
        field[z, start:start + B] = rows - product(vectors, coeffs, ((1,), (0,)))

    def up_copy(i, z):
        return remote(field.at[z, pl.ds(0, W)], inb.at[i, z], up_send.at[i, z], up_recv.at[i, z], (up, col))

    def down_copy(i, z):
        return remote(back.at[i, z], landed.at[i, z], down_send.at[i, z], down_recv.at[i, z], (down, col))

    def even(s, z):
        for g in range(2):
            apply_local(s, g, z, g * B)
            if g == 0:
                @pl.when(has_up)
                def _():
                    up_copy(s // 2, z).start()

    def straddle(s, z, send):
        i = s // 2

        @pl.when(has_down)
        def _():
            up_copy(i, z).wait_recv()
            vectors = vectors_of(s, 1)
            rows = jnp.concatenate([field[z, low:], inb[i, z]], axis=0)
            coeffs = coeffs_of(vectors, factor_of(s, 1), rows)
            bottom = (vectors[0][W:], vectors[1][W:])
            back[i, z] = rows[W:] - product(bottom, coeffs, ((1,), (0,)))
            send()
            top = (vectors[0][:W], vectors[1][:W])
            field[z, low:] = rows[:W] - product(top, coeffs, ((1,), (0,)))

    def settle(s, z):
        @pl.when(has_up)
        def _():
            up_copy(s // 2, z).wait_send()
            down_copy(s // 2, z).wait_recv()
            field[z, :W] = landed[s // 2, z]

    @pl.when(inner)
    def _():
        eig_copy = pltpu.make_async_copy(eig, field.at[0], eig_sem)
        own = [pltpu.make_async_copy(packed.at[s], buf.at[s, col], own_sem.at[s]) for s in range(steps)]

        def near(s):
            own[s].wait()

        def far(s):
            for k in range(2):
                cross(s, k).wait_recv()

        def relay(s):
            feed(s, partner).wait_recv()
            cross(s, 1).start()

        cross(0, 0).start()
        eig_copy.start()
        for copy in own:
            copy.start()
        cross(1, 0).start()
        relay(0)
        eig_copy.wait()
        relay(1)
        for s in range(2, steps):
            cross(s, 0).start()
        near(0)
        far(0)
        even(0, 0)
        near(1)
        far(1)
        straddle(1, 0, lambda: down_copy(0, 0).start())
        apply_local(1, 0, 0, W)
        settle(1, 0)
        columns.wait_recv()
        even(0, 1)
        straddle(1, 1, lambda: down_copy(0, 1).start())
        apply_local(1, 0, 1, W)
        relay(2)
        settle(1, 1)
        near(2)
        far(2)
        even(2, 1)
        relay(3)
        even(2, 0)
        near(3)

        def last_straddle():
            i = last // 2
            straddle(last, 1, lambda: result(0, back.at[i, 1], down).start())
            result(2, field.at[1, pl.ds(low, W)], row).start()
            straddle(last, 0, lambda: down_copy(i, 0).start())

            @pl.when(has_up)
            def _():
                up_copy(i, 1).wait_send()
                up_copy(i, 0).wait_send()

            @pl.when(jnp.logical_not(has_up))
            def _():
                result(0, field.at[1, pl.ds(0, W)], row).start()

        def last_local():
            apply_local(last, 0, 1, W)
            result(1, field.at[1, pl.ds(W, B)], row).start()
            apply_local(last, 0, 0, W)

        @pl.when(col == 1)
        def _():
            last_local()
            far(last)
            last_straddle()

        @pl.when(col == 2)
        def _():
            last_straddle()
            far(last)
            last_local()

        @pl.when(has_up)
        def _():
            down_copy(last // 2, 0).wait_recv()
            field[0, :W] = landed[last // 2, 0]

        store = pltpu.make_async_copy(field.at[0], out, out_sem)
        store.start()
        for s in range(steps):
            for k in range(2):
                cross(s, k).wait_send()

        @pl.when(has_down)
        def _():
            down_copy(0, 0).wait_send()
            down_copy(0, 1).wait_send()
            down_copy(last // 2, 0).wait_send()
            result(0, back.at[last // 2, 1], down).wait_send()

        @pl.when(jnp.logical_not(has_up))
        def _():
            result(0, field.at[1, pl.ds(0, W)], row).wait_send()

        result(1, field.at[1, pl.ds(W, B)], row).wait_send()
        result(2, field.at[1, pl.ds(low, W)], row).wait_send()
        store.wait()


def on_device(n, rows_n, eigvec, refl, tfac, sched):
    steps, v_rows, _ = refl.shape
    t_rows = tfac.shape[1]
    groups = sched.shape[0]
    evcount = eigvec.shape[1]
    piece = v_rows + t_rows
    hops = n // 2
    owner = lax.axis_index("col") * v_rows // B
    slots = lax.dynamic_index_in_dim(sched, owner, 0, keepdims=False)
    anywhere = pl.BlockSpec(memory_space=pl.ANY)
    packed = pl.pallas_call(
        pick_kernel,
        out_shape=jax.ShapeDtypeStruct((steps, piece, W), jnp.float32),
        in_specs=[pl.BlockSpec(memory_space=pltpu.SMEM), anywhere, anywhere],
        out_specs=anywhere,
        scratch_shapes=[
            pltpu.VMEM((steps, piece, W), jnp.float32),
            pltpu.SemaphoreType.DMA((steps, 2)),
            pltpu.SemaphoreType.DMA((steps,)),
        ],
        name="pick",
    )(slots, refl, tfac)
    half_steps = steps // 2
    if n == 4 and groups == 2 and steps == 4:
        two = (half_steps, 2)
        return pl.pallas_call(
            functools.partial(line_kernel, rows_n),
            out_shape=jax.ShapeDtypeStruct(eigvec.shape, jnp.float32),
            in_specs=[anywhere, anywhere],
            out_specs=anywhere,
            scratch_shapes=[
                pltpu.VMEM((2, *eigvec.shape), jnp.float32),
                pltpu.VMEM((steps, n, piece, W), jnp.float32),
                pltpu.VMEM((*two, W, evcount), jnp.float32),
                pltpu.VMEM((*two, W, evcount), jnp.float32),
                pltpu.VMEM((*two, W, evcount), jnp.float32),
                pltpu.SemaphoreType.DMA((steps,)),
                pltpu.SemaphoreType.DMA,
                pltpu.SemaphoreType.DMA,
                pltpu.SemaphoreType.DMA((steps,)),
                pltpu.SemaphoreType.DMA((steps,)),
                pltpu.SemaphoreType.DMA,
                pltpu.SemaphoreType.DMA,
                pltpu.SemaphoreType.DMA((steps, 2)),
                pltpu.SemaphoreType.DMA((steps, 2)),
                pltpu.SemaphoreType.DMA(two),
                pltpu.SemaphoreType.DMA(two),
                pltpu.SemaphoreType.DMA(two),
                pltpu.SemaphoreType.DMA(two),
                pltpu.SemaphoreType.DMA((3,)),
                pltpu.SemaphoreType.DMA((3,)),
            ],
            compiler_params=pltpu.CompilerParams(
                collective_id=0, has_side_effects=True, vmem_limit_bytes=48 << 20
            ),
            name="sweep",
        )(packed, eigvec)
    return pl.pallas_call(
        functools.partial(main_kernel, n, rows_n, groups),
        out_shape=jax.ShapeDtypeStruct(eigvec.shape, jnp.float32),
        in_specs=[anywhere, anywhere],
        out_specs=anywhere,
        scratch_shapes=[
            pltpu.VMEM(eigvec.shape, jnp.float32),
            pltpu.VMEM((steps, n, piece, W), jnp.float32),
            pltpu.VMEM((half_steps, W, evcount), jnp.float32),
            pltpu.VMEM((half_steps, W, evcount), jnp.float32),
            pltpu.VMEM((half_steps, W, evcount), jnp.float32),
            pltpu.SemaphoreType.DMA((steps,)),
            pltpu.SemaphoreType.DMA,
            pltpu.SemaphoreType.DMA,
            pltpu.SemaphoreType.DMA((steps, 2, hops, 2)),
            pltpu.SemaphoreType.DMA((steps, 2, hops, 2)),
            pltpu.SemaphoreType.DMA((half_steps,)),
            pltpu.SemaphoreType.DMA((half_steps,)),
            pltpu.SemaphoreType.DMA((half_steps,)),
            pltpu.SemaphoreType.DMA((half_steps,)),
        ],
        compiler_params=pltpu.CompilerParams(
            collective_id=0, has_side_effects=True, vmem_limit_bytes=48 << 20
        ),
        name="sweep",
    )(packed, eigvec)


def solution(mesh):
    placed = (
        P("row", "col"),
        P(None, ("row", "col"), None),
        P(None, ("row", "col"), None),
        P("row", None),
    )
    body = functools.partial(on_device, mesh.shape["col"], mesh.shape["row"])
    return jax.shard_map(body, mesh=mesh, in_specs=placed, out_specs=P("row", "col"), check_vma=False)
```

```python
import functools

import jax
import jax.numpy as jnp
from jax import lax
from jax.experimental import pallas as pl
from jax.experimental.pallas import tpu as pltpu
from jax.sharding import PartitionSpec as P

B = 512
W = 256
MESH = pl.DeviceIdType.MESH


def split(x):
    high = x.astype(jnp.bfloat16)
    low = (x - high.astype(jnp.float32)).astype(jnp.bfloat16)
    return high, low


def product(left, right, dims):
    def one(a, b):
        return lax.dot_general(a, b, (dims, ((), ())), preferred_element_type=jnp.float32)

    return one(left[0], right[0]) + (one(left[0], right[1]) + one(left[1], right[0]))


def pick_kernel(slots, refl, tfac, packed, hold, in_sem, out_sem):
    steps = packed.shape[0]
    v_rows = refl.shape[1]
    t_rows = tfac.shape[1]
    loads, stores = [], []
    for s in range(steps):
        slot = slots[s]
        loads.append(
            (
                pltpu.make_async_copy(refl.at[slot], hold.at[s, pl.ds(0, v_rows)], in_sem.at[s, 0]),
                pltpu.make_async_copy(tfac.at[slot], hold.at[s, pl.ds(v_rows, t_rows)], in_sem.at[s, 1]),
            )
        )
        stores.append(pltpu.make_async_copy(hold.at[s], packed.at[s], out_sem.at[s]))
    for pair in loads:
        for copy in pair:
            copy.start()
    for pair, store in zip(loads, stores):
        for copy in pair:
            copy.wait()
        store.start()
    for store in stores:
        store.wait()


def main_kernel(n, rows_n, groups, packed, eig, out, field, buf, inb, back, landed, own_sem, eig_sem, out_sem,
                ring_send, ring_recv, up_send, up_recv, down_send, down_recv):
    steps, piece, _ = packed.shape
    v_rows = groups * B // n
    per_group = n // groups
    half = piece // 2
    hops = n // 2
    row = lax.axis_index("row")
    col = lax.axis_index("col")
    right = lax.rem(col + 1, n)
    left = lax.rem(col + n - 1, n)
    has_down = row < rows_n - 1
    has_up = row > 0
    down = jnp.minimum(row + 1, rows_n - 1)
    up = jnp.maximum(row - 1, 0)

    eig_copy = pltpu.make_async_copy(eig, field, eig_sem)
    eig_copy.start()

    barrier = pltpu.get_barrier_semaphore()
    pl.semaphore_signal(barrier, inc=1, device_id=(row, left), device_id_type=MESH)
    pl.semaphore_signal(barrier, inc=1, device_id=(row, right), device_id_type=MESH)

    @pl.when(has_up)
    def _():
        pl.semaphore_signal(barrier, inc=1, device_id=(up, col), device_id_type=MESH)

    @pl.when(has_down)
    def _():
        pl.semaphore_signal(barrier, inc=1, device_id=(down, col), device_id_type=MESH)

    pl.semaphore_wait(barrier, 2 + jnp.minimum(row, 1) + jnp.minimum(rows_n - 1 - row, 1))

    def ring_copy(s, way, hop, part):
        target = right if way == 0 else left
        owner = lax.rem(col + n - hop, n) if way == 0 else lax.rem(col + hop, n)
        span = pl.ds(part * half, half)
        src = packed.at[s, span] if hop == 0 else buf.at[s, owner, span]
        return pltpu.make_async_remote_copy(
            src_ref=src,
            dst_ref=buf.at[s, owner, span],
            send_sem=ring_send.at[s, way, hop, part],
            recv_sem=ring_recv.at[s, way, hop, part],
            device_id=(row, target),
            device_id_type=MESH,
        )

    def parts_of(way, hop):
        order = (0, 1) if way == 0 else (1, 0)
        return order[:1] if hop == hops - 1 else order

    def send_own(s):
        for k in range(len(parts_of(0, 0))):
            for way in (0, 1):
                ring_copy(s, way, 0, parts_of(way, 0)[k]).start()

    def forward(s):
        for hop in range(1, hops):
            for k in range(len(parts_of(0, hop))):
                for way in (0, 1):
                    part = parts_of(way, hop)[k]
                    ring_copy(s, way, hop - 1, part).wait_recv()
                    ring_copy(s, way, hop, part).start()

    def finish(s):
        for hop in range(hops):
            for way in (0, 1):
                done = parts_of(way, hop + 1) if hop + 1 < hops else ()
                for part in parts_of(way, hop):
                    if part not in done:
                        ring_copy(s, way, hop, part).wait_recv()

    def vectors_of(s, g):
        block = buf[s, g * per_group:(g + 1) * per_group, :v_rows]
        return split(block.reshape(B, W))

    def factor_of(s, g):
        block = buf[s, g * per_group:(g + 1) * per_group, v_rows:]
        return split(block.reshape(W, W))

    def coeffs_of(s, g, vectors, rows):
        coupling = product(vectors, split(rows), ((0,), (0,)))
        return split(product(factor_of(s, g), split(coupling), ((1,), (0,))))

    def apply_local(s, g, start):
        vectors = vectors_of(s, g)
        rows = field[start:start + B]
        coeffs = coeffs_of(s, g, vectors, rows)
        field[start:start + B] = rows - product(vectors, coeffs, ((1,), (0,)))

    def up_copy(i):
        return pltpu.make_async_remote_copy(
            src_ref=field.at[pl.ds(0, W)], dst_ref=inb.at[i],
            send_sem=up_send.at[i], recv_sem=up_recv.at[i],
            device_id=(up, col), device_id_type=MESH,
        )

    def down_copy(i):
        return pltpu.make_async_remote_copy(
            src_ref=back.at[i], dst_ref=landed.at[i],
            send_sem=down_send.at[i], recv_sem=down_recv.at[i],
            device_id=(down, col), device_id_type=MESH,
        )

    low = groups * B - W

    send_own(0)
    own = [pltpu.make_async_copy(packed.at[s], buf.at[s, col], own_sem.at[s]) for s in range(steps)]
    for copy in own:
        copy.start()
    eig_copy.wait()
    for s in range(steps):
        forward(s)
        if s + 1 < steps:
            send_own(s + 1)
        own[s].wait()
        finish(s)
        i = s // 2
        if s % 2 == 0:
            for g in range(groups):
                apply_local(s, g, g * B)
                if g == 0 and s + 1 < steps:
                    @pl.when(has_up)
                    def _():
                        up_copy(i).start()
        else:
            @pl.when(has_down)
            def _():
                up_copy(i).wait_recv()
                g = groups - 1
                vectors = vectors_of(s, g)
                rows = jnp.concatenate([field[low:], inb[i]], axis=0)
                coeffs = coeffs_of(s, g, vectors, rows)
                bottom = (vectors[0][W:], vectors[1][W:])
                back[i] = rows[W:] - product(bottom, coeffs, ((1,), (0,)))
                down_copy(i).start()
                top = (vectors[0][:W], vectors[1][:W])
                field[low:] = rows[:W] - product(top, coeffs, ((1,), (0,)))

            for g in range(groups - 1):
                apply_local(s, g, W + g * B)

            @pl.when(has_up)
            def _():
                up_copy(i).wait_send()
                down_copy(i).wait_recv()
                field[:W] = landed[i]

    store = pltpu.make_async_copy(field, out, out_sem)
    store.start()
    for s in range(steps):
        for way in (0, 1):
            for hop in range(hops):
                for part in parts_of(way, hop):
                    ring_copy(s, way, hop, part).wait_send()

    @pl.when(has_down)
    def _():
        for i in range(steps // 2):
            down_copy(i).wait_send()

    store.wait()


def line_kernel(rows_n, packed, eig, out, field, buf, inb, back, landed, own_sem, eig_sem, out_sem,
                feed_send, feed_recv, cols_send, cols_recv, cross_send, cross_recv,
                up_send, up_recv, down_send, down_recv, res_send, res_recv):
    steps, piece, _ = packed.shape
    v_rows = B // 2
    low = B + W
    last = steps - 1
    row = lax.axis_index("row")
    col = lax.axis_index("col")
    inner = (col == 1) | (col == 2)
    partner = col + 1 - 2 * lax.rem(col, 2)
    other = 3 - col
    has_down = row < rows_n - 1
    has_up = row > 0
    down = jnp.minimum(row + 1, rows_n - 1)
    up = jnp.maximum(row - 1, 0)

    def remote(src, dst, send, recv, target):
        return pltpu.make_async_remote_copy(
            src_ref=src, dst_ref=dst, send_sem=send, recv_sem=recv,
            device_id=target, device_id_type=MESH,
        )

    def greet(target):
        pl.semaphore_signal(barrier, inc=1, device_id=target, device_id_type=MESH)

    barrier = pltpu.get_barrier_semaphore()
    some_up = jnp.minimum(row, 1)
    some_down = jnp.minimum(rows_n - 1 - row, 1)
    greet((row, partner))

    @pl.when(inner)
    def _():
        greet((row, other))

        @pl.when(has_up)
        def _():
            greet((up, col))

        @pl.when(has_down)
        def _():
            greet((down, col))
            greet((down, partner))

    @pl.when(jnp.logical_not(inner) & has_up)
    def _():
        greet((up, partner))

    @pl.when(inner)
    def _():
        pl.semaphore_wait(barrier, 2 + some_up + 2 * some_down)

    @pl.when(jnp.logical_not(inner))
    def _():
        pl.semaphore_wait(barrier, 1 + some_up)

    def feed(s, owner):
        return remote(packed.at[s], buf.at[s, owner], feed_send.at[s], feed_recv.at[s], (row, partner))

    def columns(g):
        span = pl.ds(g * B, B)
        return remote(eig.at[span], field.at[1, span], cols_send.at[g], cols_recv.at[g], (row, partner))

    def cross(s, k):
        owner = col if k == 0 else partner
        src = packed.at[s] if k == 0 else buf.at[s, owner]
        return remote(src, buf.at[s, owner], cross_send.at[s, k], cross_recv.at[s, k], (row, other))

    def result(part, src, target_row):
        span = (pl.ds(0, W), pl.ds(W, B), pl.ds(low, W))[part]
        return remote(src, out.at[span], res_send.at[part], res_recv.at[part], (target_row, partner))

    @pl.when(jnp.logical_not(inner))
    def _():
        feed(0, col).start()
        columns(0).start()
        feed(1, col).start()
        columns(1).start()
        for s in range(2, steps):
            feed(s, col).start()
        for s in range(steps):
            feed(s, col).wait_send()
        columns(0).wait_send()
        columns(1).wait_send()
        for part in range(3):
            rows = (W, B, W)[part]
            result(part, field.at[0, pl.ds(0, rows)], row).wait_recv()

    def vectors_of(s, g):
        return split(buf[s, 2 * g:2 * g + 2, :v_rows].reshape(B, W))

    def factor_of(s, g):
        return split(buf[s, 2 * g:2 * g + 2, v_rows:].reshape(W, W))

    def coeffs_of(vectors, factor, rows):
        coupling = product(vectors, split(rows), ((0,), (0,)))
        return split(product(factor, split(coupling), ((1,), (0,))))

    def apply_local(s, g, z, start):
        vectors = vectors_of(s, g)
        rows = field[z, start:start + B]
        coeffs = coeffs_of(vectors, factor_of(s, g), rows)
        field[z, start:start + B] = rows - product(vectors, coeffs, ((1,), (0,)))

    def up_copy(i, z):
        return remote(field.at[z, pl.ds(0, W)], inb.at[i, z], up_send.at[i, z], up_recv.at[i, z], (up, col))

    def down_copy(i, z):
        return remote(back.at[i, z], landed.at[i, z], down_send.at[i, z], down_recv.at[i, z], (down, col))

    def even(s, z):
        for g in range(2):
            apply_local(s, g, z, g * B)
            if g == 0:
                @pl.when(has_up)
                def _():
                    up_copy(s // 2, z).start()

    def straddle(s, z, send):
        i = s // 2

        @pl.when(has_down)
        def _():
            up_copy(i, z).wait_recv()
            vectors = vectors_of(s, 1)
            rows = jnp.concatenate([field[z, low:], inb[i, z]], axis=0)
            coeffs = coeffs_of(vectors, factor_of(s, 1), rows)
            bottom = (vectors[0][W:], vectors[1][W:])
            back[i, z] = rows[W:] - product(bottom, coeffs, ((1,), (0,)))
            send()
            top = (vectors[0][:W], vectors[1][:W])
            field[z, low:] = rows[:W] - product(top, coeffs, ((1,), (0,)))

    def settle(s, z):
        @pl.when(has_up)
        def _():
            up_copy(s // 2, z).wait_send()
            down_copy(s // 2, z).wait_recv()
            field[z, :W] = landed[s // 2, z]

    @pl.when(inner)
    def _():
        eig_copy = pltpu.make_async_copy(eig, field.at[0], eig_sem)
        own = [pltpu.make_async_copy(packed.at[s], buf.at[s, col], own_sem.at[s]) for s in range(steps)]

        def near(s):
            own[s].wait()

        def far(s):
            for k in range(2):
                cross(s, k).wait_recv()

        def relay(s):
            feed(s, partner).wait_recv()
            cross(s, 1).start()

        cross(0, 0).start()
        eig_copy.start()
        for copy in own:
            copy.start()
        cross(1, 0).start()
        relay(0)
        cross(2, 0).start()
        eig_copy.wait()
        near(0)
        far(0)
        even(0, 0)
        columns(0).wait_recv()
        apply_local(0, 0, 1, 0)

        @pl.when(has_up)
        def _():
            up_copy(0, 1).start()

        relay(1)
        cross(3, 0).start()
        columns(1).wait_recv()
        apply_local(0, 1, 1, B)
        near(1)
        far(1)
        straddle(1, 1, lambda: down_copy(0, 1).start())
        apply_local(1, 0, 1, W)
        relay(2)
        straddle(1, 0, lambda: down_copy(0, 0).start())
        apply_local(1, 0, 0, W)
        settle(1, 1)
        settle(1, 0)
        relay(3)
        near(2)
        far(2)
        even(2, 1)
        even(2, 0)
        near(3)

        def last_straddle():
            i = last // 2
            straddle(last, 1, lambda: result(0, back.at[i, 1], down).start())
            result(2, field.at[1, pl.ds(low, W)], row).start()
            straddle(last, 0, lambda: down_copy(i, 0).start())

            @pl.when(has_up)
            def _():
                up_copy(i, 1).wait_send()
                up_copy(i, 0).wait_send()

            @pl.when(jnp.logical_not(has_up))
            def _():
                result(0, field.at[1, pl.ds(0, W)], row).start()

        def last_local():
            apply_local(last, 0, 1, W)
            result(1, field.at[1, pl.ds(W, B)], row).start()
            apply_local(last, 0, 0, W)

        @pl.when(col == 1)
        def _():
            last_local()
            far(last)
            last_straddle()

        @pl.when(col == 2)
        def _():
            last_straddle()
            far(last)
            last_local()

        @pl.when(has_up)
        def _():
            down_copy(last // 2, 0).wait_recv()
            field[0, :W] = landed[last // 2, 0]

        store = pltpu.make_async_copy(field.at[0], out, out_sem)
        store.start()
        for s in range(steps):
            for k in range(2):
                cross(s, k).wait_send()

        @pl.when(has_down)
        def _():
            down_copy(0, 0).wait_send()
            down_copy(0, 1).wait_send()
            down_copy(last // 2, 0).wait_send()
            result(0, back.at[last // 2, 1], down).wait_send()

        @pl.when(jnp.logical_not(has_up))
        def _():
            result(0, field.at[1, pl.ds(0, W)], row).wait_send()

        result(1, field.at[1, pl.ds(W, B)], row).wait_send()
        result(2, field.at[1, pl.ds(low, W)], row).wait_send()
        store.wait()


def on_device(n, rows_n, eigvec, refl, tfac, sched):
    steps, v_rows, _ = refl.shape
    t_rows = tfac.shape[1]
    groups = sched.shape[0]
    evcount = eigvec.shape[1]
    piece = v_rows + t_rows
    hops = n // 2
    owner = lax.axis_index("col") * v_rows // B
    slots = lax.dynamic_index_in_dim(sched, owner, 0, keepdims=False)
    anywhere = pl.BlockSpec(memory_space=pl.ANY)
    packed = pl.pallas_call(
        pick_kernel,
        out_shape=jax.ShapeDtypeStruct((steps, piece, W), jnp.float32),
        in_specs=[pl.BlockSpec(memory_space=pltpu.SMEM), anywhere, anywhere],
        out_specs=anywhere,
        scratch_shapes=[
            pltpu.VMEM((steps, piece, W), jnp.float32),
            pltpu.SemaphoreType.DMA((steps, 2)),
            pltpu.SemaphoreType.DMA((steps,)),
        ],
        name="pick",
    )(slots, refl, tfac)
    half_steps = steps // 2
    if n == 4 and groups == 2 and steps == 4:
        two = (half_steps, 2)
        return pl.pallas_call(
            functools.partial(line_kernel, rows_n),
            out_shape=jax.ShapeDtypeStruct(eigvec.shape, jnp.float32),
            in_specs=[anywhere, anywhere],
            out_specs=anywhere,
            scratch_shapes=[
                pltpu.VMEM((2, *eigvec.shape), jnp.float32),
                pltpu.VMEM((steps, n, piece, W), jnp.float32),
                pltpu.VMEM((*two, W, evcount), jnp.float32),
                pltpu.VMEM((*two, W, evcount), jnp.float32),
                pltpu.VMEM((*two, W, evcount), jnp.float32),
                pltpu.SemaphoreType.DMA((steps,)),
                pltpu.SemaphoreType.DMA,
                pltpu.SemaphoreType.DMA,
                pltpu.SemaphoreType.DMA((steps,)),
                pltpu.SemaphoreType.DMA((steps,)),
                pltpu.SemaphoreType.DMA((2,)),
                pltpu.SemaphoreType.DMA((2,)),
                pltpu.SemaphoreType.DMA((steps, 2)),
                pltpu.SemaphoreType.DMA((steps, 2)),
                pltpu.SemaphoreType.DMA(two),
                pltpu.SemaphoreType.DMA(two),
                pltpu.SemaphoreType.DMA(two),
                pltpu.SemaphoreType.DMA(two),
                pltpu.SemaphoreType.DMA((3,)),
                pltpu.SemaphoreType.DMA((3,)),
            ],
            compiler_params=pltpu.CompilerParams(
                collective_id=0, has_side_effects=True, vmem_limit_bytes=48 << 20
            ),
            name="sweep",
        )(packed, eigvec)
    return pl.pallas_call(
        functools.partial(main_kernel, n, rows_n, groups),
        out_shape=jax.ShapeDtypeStruct(eigvec.shape, jnp.float32),
        in_specs=[anywhere, anywhere],
        out_specs=anywhere,
        scratch_shapes=[
            pltpu.VMEM(eigvec.shape, jnp.float32),
            pltpu.VMEM((steps, n, piece, W), jnp.float32),
            pltpu.VMEM((half_steps, W, evcount), jnp.float32),
            pltpu.VMEM((half_steps, W, evcount), jnp.float32),
            pltpu.VMEM((half_steps, W, evcount), jnp.float32),
            pltpu.SemaphoreType.DMA((steps,)),
            pltpu.SemaphoreType.DMA,
            pltpu.SemaphoreType.DMA,
            pltpu.SemaphoreType.DMA((steps, 2, hops, 2)),
            pltpu.SemaphoreType.DMA((steps, 2, hops, 2)),
            pltpu.SemaphoreType.DMA((half_steps,)),
            pltpu.SemaphoreType.DMA((half_steps,)),
            pltpu.SemaphoreType.DMA((half_steps,)),
            pltpu.SemaphoreType.DMA((half_steps,)),
        ],
        compiler_params=pltpu.CompilerParams(
            collective_id=0, has_side_effects=True, vmem_limit_bytes=48 << 20
        ),
        name="sweep",
    )(packed, eigvec)


def solution(mesh):
    placed = (
        P("row", "col"),
        P(None, ("row", "col"), None),
        P(None, ("row", "col"), None),
        P("row", None),
    )
    body = functools.partial(on_device, mesh.shape["col"], mesh.shape["row"])
    return jax.shard_map(body, mesh=mesh, in_specs=placed, out_specs=P("row", "col"), check_vma=False)
```

```python
import functools

import jax
import jax.numpy as jnp
from jax import lax
from jax.experimental import pallas as pl
from jax.experimental.pallas import tpu as pltpu
from jax.sharding import PartitionSpec as P

B = 512
W = 256
MESH = pl.DeviceIdType.MESH


def split(x):
    high = x.astype(jnp.bfloat16)
    low = (x - high.astype(jnp.float32)).astype(jnp.bfloat16)
    return high, low


def product(left, right, dims):
    def one(a, b):
        return lax.dot_general(a, b, (dims, ((), ())), preferred_element_type=jnp.float32)

    return one(left[0], right[0]) + (one(left[0], right[1]) + one(left[1], right[0]))


def pick_kernel(slots, refl, tfac, packed, hold, in_sem, out_sem):
    steps = packed.shape[0]
    v_rows = refl.shape[1]
    t_rows = tfac.shape[1]
    loads, stores = [], []
    for s in range(steps):
        slot = slots[s]
        loads.append(
            (
                pltpu.make_async_copy(refl.at[slot], hold.at[s, pl.ds(0, v_rows)], in_sem.at[s, 0]),
                pltpu.make_async_copy(tfac.at[slot], hold.at[s, pl.ds(v_rows, t_rows)], in_sem.at[s, 1]),
            )
        )
        stores.append(pltpu.make_async_copy(hold.at[s], packed.at[s], out_sem.at[s]))
    for pair in loads:
        for copy in pair:
            copy.start()
    for pair, store in zip(loads, stores):
        for copy in pair:
            copy.wait()
        store.start()
    for store in stores:
        store.wait()


def main_kernel(n, rows_n, groups, packed, eig, out, field, buf, inb, back, landed, own_sem, eig_sem, out_sem,
                ring_send, ring_recv, up_send, up_recv, down_send, down_recv):
    steps, piece, _ = packed.shape
    v_rows = groups * B // n
    per_group = n // groups
    half = piece // 2
    hops = n // 2
    row = lax.axis_index("row")
    col = lax.axis_index("col")
    right = lax.rem(col + 1, n)
    left = lax.rem(col + n - 1, n)
    has_down = row < rows_n - 1
    has_up = row > 0
    down = jnp.minimum(row + 1, rows_n - 1)
    up = jnp.maximum(row - 1, 0)

    eig_copy = pltpu.make_async_copy(eig, field, eig_sem)
    eig_copy.start()

    barrier = pltpu.get_barrier_semaphore()
    pl.semaphore_signal(barrier, inc=1, device_id=(row, left), device_id_type=MESH)
    pl.semaphore_signal(barrier, inc=1, device_id=(row, right), device_id_type=MESH)

    @pl.when(has_up)
    def _():
        pl.semaphore_signal(barrier, inc=1, device_id=(up, col), device_id_type=MESH)

    @pl.when(has_down)
    def _():
        pl.semaphore_signal(barrier, inc=1, device_id=(down, col), device_id_type=MESH)

    pl.semaphore_wait(barrier, 2 + jnp.minimum(row, 1) + jnp.minimum(rows_n - 1 - row, 1))

    def ring_copy(s, way, hop, part):
        target = right if way == 0 else left
        owner = lax.rem(col + n - hop, n) if way == 0 else lax.rem(col + hop, n)
        span = pl.ds(part * half, half)
        src = packed.at[s, span] if hop == 0 else buf.at[s, owner, span]
        return pltpu.make_async_remote_copy(
            src_ref=src,
            dst_ref=buf.at[s, owner, span],
            send_sem=ring_send.at[s, way, hop, part],
            recv_sem=ring_recv.at[s, way, hop, part],
            device_id=(row, target),
            device_id_type=MESH,
        )

    def parts_of(way, hop):
        order = (0, 1) if way == 0 else (1, 0)
        return order[:1] if hop == hops - 1 else order

    def send_own(s):
        for k in range(len(parts_of(0, 0))):
            for way in (0, 1):
                ring_copy(s, way, 0, parts_of(way, 0)[k]).start()

    def forward(s):
        for hop in range(1, hops):
            for k in range(len(parts_of(0, hop))):
                for way in (0, 1):
                    part = parts_of(way, hop)[k]
                    ring_copy(s, way, hop - 1, part).wait_recv()
                    ring_copy(s, way, hop, part).start()

    def finish(s):
        for hop in range(hops):
            for way in (0, 1):
                done = parts_of(way, hop + 1) if hop + 1 < hops else ()
                for part in parts_of(way, hop):
                    if part not in done:
                        ring_copy(s, way, hop, part).wait_recv()

    def vectors_of(s, g):
        block = buf[s, g * per_group:(g + 1) * per_group, :v_rows]
        return split(block.reshape(B, W))

    def factor_of(s, g):
        block = buf[s, g * per_group:(g + 1) * per_group, v_rows:]
        return split(block.reshape(W, W))

    def coeffs_of(s, g, vectors, rows):
        coupling = product(vectors, split(rows), ((0,), (0,)))
        return split(product(factor_of(s, g), split(coupling), ((1,), (0,))))

    def apply_local(s, g, start):
        vectors = vectors_of(s, g)
        rows = field[start:start + B]
        coeffs = coeffs_of(s, g, vectors, rows)
        field[start:start + B] = rows - product(vectors, coeffs, ((1,), (0,)))

    def up_copy(i):
        return pltpu.make_async_remote_copy(
            src_ref=field.at[pl.ds(0, W)], dst_ref=inb.at[i],
            send_sem=up_send.at[i], recv_sem=up_recv.at[i],
            device_id=(up, col), device_id_type=MESH,
        )

    def down_copy(i):
        return pltpu.make_async_remote_copy(
            src_ref=back.at[i], dst_ref=landed.at[i],
            send_sem=down_send.at[i], recv_sem=down_recv.at[i],
            device_id=(down, col), device_id_type=MESH,
        )

    low = groups * B - W

    send_own(0)
    own = [pltpu.make_async_copy(packed.at[s], buf.at[s, col], own_sem.at[s]) for s in range(steps)]
    for copy in own:
        copy.start()
    eig_copy.wait()
    for s in range(steps):
        forward(s)
        if s + 1 < steps:
            send_own(s + 1)
        own[s].wait()
        finish(s)
        i = s // 2
        if s % 2 == 0:
            for g in range(groups):
                apply_local(s, g, g * B)
                if g == 0 and s + 1 < steps:
                    @pl.when(has_up)
                    def _():
                        up_copy(i).start()
        else:
            @pl.when(has_down)
            def _():
                up_copy(i).wait_recv()
                g = groups - 1
                vectors = vectors_of(s, g)
                rows = jnp.concatenate([field[low:], inb[i]], axis=0)
                coeffs = coeffs_of(s, g, vectors, rows)
                bottom = (vectors[0][W:], vectors[1][W:])
                back[i] = rows[W:] - product(bottom, coeffs, ((1,), (0,)))
                down_copy(i).start()
                top = (vectors[0][:W], vectors[1][:W])
                field[low:] = rows[:W] - product(top, coeffs, ((1,), (0,)))

            for g in range(groups - 1):
                apply_local(s, g, W + g * B)

            @pl.when(has_up)
            def _():
                up_copy(i).wait_send()
                down_copy(i).wait_recv()
                field[:W] = landed[i]

    store = pltpu.make_async_copy(field, out, out_sem)
    store.start()
    for s in range(steps):
        for way in (0, 1):
            for hop in range(hops):
                for part in parts_of(way, hop):
                    ring_copy(s, way, hop, part).wait_send()

    @pl.when(has_down)
    def _():
        for i in range(steps // 2):
            down_copy(i).wait_send()

    store.wait()


def line_kernel(rows_n, packed, eig, out, field, buf, inb, back, landed, own_sem, eig_sem, out_sem,
                feed_send, feed_recv, cols_send, cols_recv, cross_send, cross_recv,
                up_send, up_recv, down_send, down_recv, res_send, res_recv):
    steps, piece, _ = packed.shape
    v_rows = B // 2
    low = B + W
    last = steps - 1
    row = lax.axis_index("row")
    col = lax.axis_index("col")
    inner = (col == 1) | (col == 2)
    partner = col + 1 - 2 * lax.rem(col, 2)
    other = 3 - col
    has_down = row < rows_n - 1
    has_up = row > 0
    down = jnp.minimum(row + 1, rows_n - 1)
    up = jnp.maximum(row - 1, 0)

    def remote(src, dst, send, recv, target):
        return pltpu.make_async_remote_copy(
            src_ref=src, dst_ref=dst, send_sem=send, recv_sem=recv,
            device_id=target, device_id_type=MESH,
        )

    def greet(target):
        pl.semaphore_signal(barrier, inc=1, device_id=target, device_id_type=MESH)

    barrier = pltpu.get_barrier_semaphore()
    some_up = jnp.minimum(row, 1)
    some_down = jnp.minimum(rows_n - 1 - row, 1)
    greet((row, partner))

    @pl.when(inner)
    def _():
        greet((row, other))

        @pl.when(has_up)
        def _():
            greet((up, col))

        @pl.when(has_down)
        def _():
            greet((down, col))
            greet((down, partner))

    @pl.when(jnp.logical_not(inner) & has_up)
    def _():
        greet((up, partner))

    @pl.when(inner)
    def _():
        pl.semaphore_wait(barrier, 2 + some_up + 2 * some_down)

    @pl.when(jnp.logical_not(inner))
    def _():
        pl.semaphore_wait(barrier, 1 + some_up)

    def feed(s, owner):
        return remote(packed.at[s], buf.at[s, owner], feed_send.at[s], feed_recv.at[s], (row, partner))

    def columns(g):
        span = pl.ds(g * B, B)
        return remote(eig.at[span], field.at[1, span], cols_send.at[g], cols_recv.at[g], (row, partner))

    def cross(s, k):
        owner = col if k == 0 else partner
        src = packed.at[s] if k == 0 else buf.at[s, owner]
        return remote(src, buf.at[s, owner], cross_send.at[s, k], cross_recv.at[s, k], (row, other))

    def result(part, src, target_row):
        span = (pl.ds(0, W), pl.ds(W, B), pl.ds(low, W))[part]
        return remote(src, out.at[span], res_send.at[part], res_recv.at[part], (target_row, partner))

    @pl.when(jnp.logical_not(inner))
    def _():
        feed(0, col).start()
        columns(0).start()
        feed(1, col).start()
        feed(2, col).start()
        columns(1).start()
        feed(3, col).start()
        for s in range(steps):
            feed(s, col).wait_send()
        columns(0).wait_send()
        columns(1).wait_send()
        for part in range(3):
            rows = (W, B, W)[part]
            result(part, field.at[0, pl.ds(0, rows)], row).wait_recv()

    def vectors_of(s, g):
        return split(buf[s, 2 * g:2 * g + 2, :v_rows].reshape(B, W))

    def factor_of(s, g):
        return split(buf[s, 2 * g:2 * g + 2, v_rows:].reshape(W, W))

    def coeffs_of(vectors, factor, rows):
        coupling = product(vectors, split(rows), ((0,), (0,)))
        return split(product(factor, split(coupling), ((1,), (0,))))

    def apply_local(s, g, z, start):
        vectors = vectors_of(s, g)
        rows = field[z, start:start + B]
        coeffs = coeffs_of(vectors, factor_of(s, g), rows)
        field[z, start:start + B] = rows - product(vectors, coeffs, ((1,), (0,)))

    def up_copy(i, z):
        return remote(field.at[z, pl.ds(0, W)], inb.at[i, z], up_send.at[i, z], up_recv.at[i, z], (up, col))

    def down_copy(i, z):
        return remote(back.at[i, z], landed.at[i, z], down_send.at[i, z], down_recv.at[i, z], (down, col))

    def even(s, z):
        for g in range(2):
            apply_local(s, g, z, g * B)
            if g == 0:
                @pl.when(has_up)
                def _():
                    up_copy(s // 2, z).start()

    def straddle(s, z, send):
        i = s // 2

        @pl.when(has_down)
        def _():
            up_copy(i, z).wait_recv()
            vectors = vectors_of(s, 1)
            rows = jnp.concatenate([field[z, low:], inb[i, z]], axis=0)
            coeffs = coeffs_of(vectors, factor_of(s, 1), rows)
            bottom = (vectors[0][W:], vectors[1][W:])
            back[i, z] = rows[W:] - product(bottom, coeffs, ((1,), (0,)))
            send()
            top = (vectors[0][:W], vectors[1][:W])
            field[z, low:] = rows[:W] - product(top, coeffs, ((1,), (0,)))

    def settle(s, z):
        @pl.when(has_up)
        def _():
            up_copy(s // 2, z).wait_send()
            down_copy(s // 2, z).wait_recv()
            field[z, :W] = landed[s // 2, z]

    @pl.when(inner)
    def _():
        eig_copy = pltpu.make_async_copy(eig, field.at[0], eig_sem)
        own = [pltpu.make_async_copy(packed.at[s], buf.at[s, col], own_sem.at[s]) for s in range(steps)]

        def near(s):
            own[s].wait()

        def far(s):
            for k in range(2):
                cross(s, k).wait_recv()

        def relay(s):
            feed(s, partner).wait_recv()
            cross(s, 1).start()

        cross(0, 0).start()
        eig_copy.start()
        for copy in own:
            copy.start()
        cross(1, 0).start()
        relay(0)
        cross(2, 0).start()
        eig_copy.wait()
        near(0)
        far(0)
        even(0, 0)
        columns(0).wait_recv()
        apply_local(0, 0, 1, 0)

        @pl.when(has_up)
        def _():
            up_copy(0, 1).start()

        relay(1)
        relay(2)
        cross(3, 0).start()
        near(1)
        far(1)
        straddle(1, 0, lambda: down_copy(0, 0).start())
        apply_local(1, 0, 0, W)
        columns(1).wait_recv()
        apply_local(0, 1, 1, B)
        straddle(1, 1, lambda: down_copy(0, 1).start())
        apply_local(1, 0, 1, W)
        settle(1, 0)
        settle(1, 1)

        @pl.when(lax.rem(row, 2) == 0)
        def _():
            relay(3)

        near(2)
        far(2)
        even(2, 1)

        @pl.when(lax.rem(row, 2) == 1)
        def _():
            relay(3)

        even(2, 0)
        near(3)

        def last_straddle():
            i = last // 2
            straddle(last, 1, lambda: result(0, back.at[i, 1], down).start())
            result(2, field.at[1, pl.ds(low, W)], row).start()
            straddle(last, 0, lambda: down_copy(i, 0).start())

            @pl.when(has_up)
            def _():
                up_copy(i, 1).wait_send()
                up_copy(i, 0).wait_send()

            @pl.when(jnp.logical_not(has_up))
            def _():
                result(0, field.at[1, pl.ds(0, W)], row).start()

        def last_local():
            apply_local(last, 0, 1, W)
            result(1, field.at[1, pl.ds(W, B)], row).start()
            apply_local(last, 0, 0, W)

        @pl.when(col == 1)
        def _():
            last_local()
            far(last)
            last_straddle()

        @pl.when(col == 2)
        def _():
            last_straddle()
            far(last)
            last_local()

        @pl.when(has_up)
        def _():
            down_copy(last // 2, 0).wait_recv()
            field[0, :W] = landed[last // 2, 0]

        store = pltpu.make_async_copy(field.at[0], out, out_sem)
        store.start()
        for s in range(steps):
            for k in range(2):
                cross(s, k).wait_send()

        @pl.when(has_down)
        def _():
            down_copy(0, 0).wait_send()
            down_copy(0, 1).wait_send()
            down_copy(last // 2, 0).wait_send()
            result(0, back.at[last // 2, 1], down).wait_send()

        @pl.when(jnp.logical_not(has_up))
        def _():
            result(0, field.at[1, pl.ds(0, W)], row).wait_send()

        result(1, field.at[1, pl.ds(W, B)], row).wait_send()
        result(2, field.at[1, pl.ds(low, W)], row).wait_send()
        store.wait()


def on_device(n, rows_n, eigvec, refl, tfac, sched):
    steps, v_rows, _ = refl.shape
    t_rows = tfac.shape[1]
    groups = sched.shape[0]
    evcount = eigvec.shape[1]
    piece = v_rows + t_rows
    hops = n // 2
    owner = lax.axis_index("col") * v_rows // B
    slots = lax.dynamic_index_in_dim(sched, owner, 0, keepdims=False)
    anywhere = pl.BlockSpec(memory_space=pl.ANY)
    packed = pl.pallas_call(
        pick_kernel,
        out_shape=jax.ShapeDtypeStruct((steps, piece, W), jnp.float32),
        in_specs=[pl.BlockSpec(memory_space=pltpu.SMEM), anywhere, anywhere],
        out_specs=anywhere,
        scratch_shapes=[
            pltpu.VMEM((steps, piece, W), jnp.float32),
            pltpu.SemaphoreType.DMA((steps, 2)),
            pltpu.SemaphoreType.DMA((steps,)),
        ],
        name="pick",
    )(slots, refl, tfac)
    half_steps = steps // 2
    if n == 4 and groups == 2 and steps == 4:
        two = (half_steps, 2)
        return pl.pallas_call(
            functools.partial(line_kernel, rows_n),
            out_shape=jax.ShapeDtypeStruct(eigvec.shape, jnp.float32),
            in_specs=[anywhere, anywhere],
            out_specs=anywhere,
            scratch_shapes=[
                pltpu.VMEM((2, *eigvec.shape), jnp.float32),
                pltpu.VMEM((steps, n, piece, W), jnp.float32),
                pltpu.VMEM((*two, W, evcount), jnp.float32),
                pltpu.VMEM((*two, W, evcount), jnp.float32),
                pltpu.VMEM((*two, W, evcount), jnp.float32),
                pltpu.SemaphoreType.DMA((steps,)),
                pltpu.SemaphoreType.DMA,
                pltpu.SemaphoreType.DMA,
                pltpu.SemaphoreType.DMA((steps,)),
                pltpu.SemaphoreType.DMA((steps,)),
                pltpu.SemaphoreType.DMA((2,)),
                pltpu.SemaphoreType.DMA((2,)),
                pltpu.SemaphoreType.DMA((steps, 2)),
                pltpu.SemaphoreType.DMA((steps, 2)),
                pltpu.SemaphoreType.DMA(two),
                pltpu.SemaphoreType.DMA(two),
                pltpu.SemaphoreType.DMA(two),
                pltpu.SemaphoreType.DMA(two),
                pltpu.SemaphoreType.DMA((3,)),
                pltpu.SemaphoreType.DMA((3,)),
            ],
            compiler_params=pltpu.CompilerParams(
                collective_id=0, has_side_effects=True, vmem_limit_bytes=48 << 20
            ),
            name="sweep",
        )(packed, eigvec)
    return pl.pallas_call(
        functools.partial(main_kernel, n, rows_n, groups),
        out_shape=jax.ShapeDtypeStruct(eigvec.shape, jnp.float32),
        in_specs=[anywhere, anywhere],
        out_specs=anywhere,
        scratch_shapes=[
            pltpu.VMEM(eigvec.shape, jnp.float32),
            pltpu.VMEM((steps, n, piece, W), jnp.float32),
            pltpu.VMEM((half_steps, W, evcount), jnp.float32),
            pltpu.VMEM((half_steps, W, evcount), jnp.float32),
            pltpu.VMEM((half_steps, W, evcount), jnp.float32),
            pltpu.SemaphoreType.DMA((steps,)),
            pltpu.SemaphoreType.DMA,
            pltpu.SemaphoreType.DMA,
            pltpu.SemaphoreType.DMA((steps, 2, hops, 2)),
            pltpu.SemaphoreType.DMA((steps, 2, hops, 2)),
            pltpu.SemaphoreType.DMA((half_steps,)),
            pltpu.SemaphoreType.DMA((half_steps,)),
            pltpu.SemaphoreType.DMA((half_steps,)),
            pltpu.SemaphoreType.DMA((half_steps,)),
        ],
        compiler_params=pltpu.CompilerParams(
            collective_id=0, has_side_effects=True, vmem_limit_bytes=48 << 20
        ),
        name="sweep",
    )(packed, eigvec)


def solution(mesh):
    placed = (
        P("row", "col"),
        P(None, ("row", "col"), None),
        P(None, ("row", "col"), None),
        P("row", None),
    )
    body = functools.partial(on_device, mesh.shape["col"], mesh.shape["row"])
    return jax.shard_map(body, mesh=mesh, in_specs=placed, out_specs=P("row", "col"), check_vma=False)
```
